256 devices in a mesh: row: 32 (over y, x, core), col: 8 (over z).
Axes of the slice: x: 4, y: 4, z: 8, core: 2. Of those that a mesh axis runs over, the one named last changes fastest.
Arguments:
- inputs: bfloat16 [4096, 5120], P('row', 'col'), may hold values from -6 to 6
- grad_out: bfloat16 [4096, 5120], P('row', 'col'), may hold values from -6 to 6
- pre_act: bfloat16 [4096, 13824], P('col', 'row'), may hold values from -6 to 6
- w_in: bfloat16 [13824, 5120], P('row', 'col'), may hold values from -0.078125 to 0.078125
- w_out: bfloat16 [13824, 5120], P('row', 'col'), may hold values from -0.0546875 to 0.0546875
- row_in_prev: float32 [13824], P('row'), may hold values from 204.8 to 24576, as said below
- col_in_prev: float32 [5120], P('col'), may hold values from 204.8 to 24576, as said below
- row_out_prev: float32 [13824], P('row'), may hold values from 204.8 to 24576, as said below
- col_out_prev: float32 [5120], P('col'), may hold values from 204.8 to 24576, as said below
Outputs:
- input_grad: bfloat16 [4096, 5120], P('row', 'col')
- update_in: float32 [13824, 5120], P('row', 'col')
- row_in: float32 [13824], P('row')
- col_in: float32 [5120], P('col')
- update_out: float32 [13824, 5120], P('row', 'col')
- row_out: float32 [13824], P('row')
- col_out: float32 [5120], P('col')
The draws below stay inside these ranges and needn't reach their ends.
Inputs may be any that keep to these rules, and one draw needn't show every extreme that they name: `row_in_prev`: positive. `col_in_prev`: positive. `row_out_prev`: positive. `col_out_prev`: positive.
All inputs are finite; a program needn't handle non-finite values.
Results may differ from the reference program's by a relative error of at most 0.023.
Values may be sent and summed in bfloat16 or wider, within the bound.
A program may use at most 128 MiB of HBM per device.

```python
import math
import jax
import jax.numpy as jnp
from jax import lax

D = 5120
FF = 13824
TOKENS = 4096
N_ROW = 32


def falling_moments(key, salt, length):
    key = jax.random.fold_in(key, salt)
    position = jnp.arange(length).astype(jnp.float32) / length
    spread = jax.random.uniform(key, (length,), jnp.float32, jnp.log(0.5), jnp.log(2.0))
    factor = 10.0
    return TOKENS * jnp.exp(spread) * 3.0 * jnp.exp(-jnp.log(factor) * position)


def draw_row_in_prev(key, part):
    return falling_moments(key, 11, FF)


def draw_col_in_prev(key, part):
    return falling_moments(key, 23, D)


def draw_row_out_prev(key, part):
    return falling_moments(key, 37, FF)


def draw_col_out_prev(key, part):
    return falling_moments(key, 41, D)


def levels(stream_key, extent, split, least, largest):
    def one(axis_at, parts):
        heights = jax.random.uniform(jax.random.fold_in(jax.random.fold_in(stream_key, 6), axis_at), (parts,), jnp.float32, least / len(split), largest / len(split))
        return jnp.repeat(jnp.exp(heights), extent[axis_at] // parts).reshape((-1,) + (1,) * (len(extent) - axis_at - 1))

    gain = one(*split[0])
    for cut in split[1:]:
        gain = gain * one(*cut)
    return gain


def gaussian(rng, dims, scale, reach, cuts=(), kind=jnp.bfloat16):
    result = jax.random.normal(rng, dims, jnp.float32) * scale
    if len(cuts) > 0:
        result = levels(rng, dims, cuts, -0.22, 0.18) * result
    return jnp.clip(result, min=-reach, max=reach).astype(kind)


def setup_inputs(seed: int = 0) -> dict:
    seeds = jax.random.split(jax.random.key(seed), 10)
    inputs = gaussian(seeds[0], (TOKENS, D), 1.0, 6.0, ((0, 32), (1, 8)))
    grad_out = gaussian(seeds[1], (TOKENS, D), 1.0, 6.0, ((0, 32), (1, 8)))
    pre_act = gaussian(seeds[2], (TOKENS, FF), 1.0, 6.0, ((0, 8), (1, 32)))
    w_in = gaussian(seeds[3], (FF, D), D ** -0.5, 0.078125, ((0, 32), (1, 8)))
    w_out = gaussian(seeds[4], (FF, D), FF ** -0.5, 0.0546875, ((0, 32), (1, 8)))
    row_in_prev = draw_row_in_prev(jax.random.fold_in(seeds[9], 71), 0)
    col_in_prev = draw_col_in_prev(jax.random.fold_in(seeds[9], 71), 0)
    row_out_prev = draw_row_out_prev(jax.random.fold_in(seeds[9], 71), 0)
    col_out_prev = draw_col_out_prev(jax.random.fold_in(seeds[9], 71), 0)
    return {"inputs": inputs, "grad_out": grad_out, "pre_act": pre_act, "w_in": w_in, "w_out": w_out, "row_in_prev": row_in_prev, "col_in_prev": col_in_prev, "row_out_prev": row_out_prev, "col_out_prev": col_out_prev}


decay_rate = 0.8
epsilon_sq = 1e-30
clip_limit = 0.25
gelu_coef = 0.044715
root_coef = math.sqrt(2.0 / math.pi)

def gelu_parts(pre_float):
    tanh_value = jnp.tanh(root_coef * (pre_float + gelu_coef * pre_float * pre_float * pre_float))
    value = 0.5 * pre_float * (1.0 + tanh_value)
    slope = 0.5 * (1.0 + tanh_value) + 0.5 * pre_float * (1.0 - tanh_value * tanh_value) * root_coef * (1.0 + 3.0 * gelu_coef * pre_float * pre_float)
    return (value, slope)

def adafactor(gradient, row_prev, col_prev):
    square = gradient * gradient
    row_next = decay_rate * row_prev + (1.0 - decay_rate) * (lax.optimization_barrier(jnp.sum(square, axis=1)) / D + epsilon_sq)
    col_next = decay_rate * col_prev + (1.0 - decay_rate) * (lax.optimization_barrier(jnp.sum(square, axis=0)) / FF + epsilon_sq)
    raw = gradient / jnp.sqrt(row_next[:, None] * col_next[None, :] / TOKENS)
    rms_value = jnp.sqrt(jnp.sum(raw * raw) / (FF * D))
    return (raw / jnp.maximum(1.0, rms_value / clip_limit), row_next, col_next)

def reference(inputs, grad_out, pre_act, w_in, w_out, row_in_prev, col_in_prev, row_out_prev, col_out_prev):
    value, slope = gelu_parts(pre_act.astype(jnp.float32))
    act = value.astype(jnp.bfloat16)
    hidden_grad = jnp.dot(grad_out, w_out.T, preferred_element_type=jnp.float32)
    pre_grad = (hidden_grad * slope).astype(jnp.bfloat16)
    grad_w_out = jnp.dot(act.T, grad_out, preferred_element_type=jnp.float32)
    grad_w_in = jnp.dot(pre_grad.T, inputs, preferred_element_type=jnp.float32)
    block_rows = FF // N_ROW
    hidden_blocks = pre_grad.reshape(TOKENS, N_ROW, block_rows).transpose(1, 0, 2)
    weight_blocks = w_in.reshape(N_ROW, block_rows, D)

    def add_block(total, pair):
        term = jnp.dot(pair[0], pair[1], preferred_element_type=jnp.float32).astype(jnp.bfloat16)
        term = lax.optimization_barrier(term)
        return (total + term.astype(jnp.float32), None)
    summed, _ = lax.scan(add_block, jnp.zeros((TOKENS, D), jnp.float32), (hidden_blocks, weight_blocks))
    input_grad = summed.astype(jnp.bfloat16)
    update_in, row_in, col_in = adafactor(grad_w_in, row_in_prev, col_in_prev)
    update_out, row_out, col_out = adafactor(grad_w_out, row_out_prev, col_out_prev)
    return (input_grad, update_in, row_in, col_in, update_out, row_out, col_out)
```

```python
import math

import jax
import jax.numpy as jnp
from jax import lax
from jax.experimental import pallas as pl
from jax.experimental.pallas import tpu as pltpu
from jax.sharding import PartitionSpec as P

D = 5120
FF = 13824
TOKENS = 4096
NY, NX, NK, NZ = 4, 4, 2, 8
TB = 128
FB = 432
DB = 640
HALF = DB // 2
QUART = DB // 4
EIGHTH = DB // 8

decay_rate = 0.8
epsilon_sq = 1e-30
clip_limit = 0.25
gelu_coef = 0.044715
root_coef = math.sqrt(2.0 / math.pi)

MESH = pl.DeviceIdType.MESH
bf16 = jnp.bfloat16
f32 = jnp.float32


def gelu_parts(p):
    t = jnp.tanh(root_coef * (p + gelu_coef * p * p * p))
    value = 0.5 * p * (1.0 + t)
    slope = 0.5 * (1.0 + t) + 0.5 * p * (1.0 - t * t) * root_coef * (
        1.0 + 3.0 * gelu_coef * p * p
    )
    return value, slope


def dot_nt(a, b):
    return lax.dot_general(a, b, (((1,), (1,)), ((), ())), preferred_element_type=f32)


def dot_nn(a, b):
    return lax.dot_general(a, b, (((1,), (0,)), ((), ())), preferred_element_type=f32)


def ring_length(h, d):
    return 4 if (h == 0) == (d == 0) else 3


SIGN = (1, -1)


def kernel(
    x_ref, g_ref, pre_ref, win_ref, wout_ref, rip_ref, cip_ref, rop_ref, cop_ref,
    ig_ref, ui_ref, ri_ref, ci_ref, uo_ref, ro_ref, co_ref,
    g_all, x_all, act_all, p_all, slope_s, hp, rs_buf, wt_s, tr_s,
    acc_out, acc_in, ipart, sib_buf, y_u, y_v, y_p, y_m, x_u, x_v, x_p, x_m,
    a2u, a2v, a2p, a2m, b2u, b2v, b2p, b2m, fin_buf, out_s,
    row_st, row_rx, prev_s, col_st, col_rx, col2_st, col2_rx,
    sc_st, sc2_st, sc3_st, sc_rx1, sc_rx2, sc_rx3,
    ssem, rsem, sib_ss, sib_rs,
):
    r = lax.axis_index("row")
    z = lax.axis_index("col")
    y = r // 8
    x = (r // 2) % 4
    k = r % 2

    def dev(yy, xx, kk, zz):
        return ((yy * 4 + xx) * 2 + kk, zz)

    def yo(o):
        return (y + (o + 4)) % 4

    def xo(o):
        return (x + (o + 4)) % 4

    def zo(o):
        return (z + (o + 8)) % 8

    sib = dev(y, x, 1 - k, z)
    xdev = {1: dev(y, xo(1), k, z), -1: dev(y, xo(-1), k, z)}
    ydev = {1: dev(yo(1), x, k, z), -1: dev(yo(-1), x, k, z)}
    zdev = {1: dev(y, x, k, zo(1)), -1: dev(y, x, k, zo(-1))}
    xk_peers = [dev(y, xo(o // 2), (k + o) % 2, z) for o in range(1, 8)]
    y_peers = [dev(yo(o), x, k, z) for o in range(1, 4)]
    z_peers = [dev(y, x, k, zo(o)) for o in range(1, 8)]

    barrier = pltpu.get_barrier_semaphore()
    everyone = xk_peers + y_peers + z_peers
    for p in everyone:
        pl.semaphore_signal(barrier, inc=1, device_id=p, device_id_type=MESH)

    count = [0]
    sent = []

    def start(src, dst, peer):
        i = count[0]
        count[0] += 1
        cp = pltpu.make_async_remote_copy(
            src_ref=src, dst_ref=dst, send_sem=ssem.at[i], recv_sem=rsem.at[i],
            device_id=peer, device_id_type=MESH,
        )
        cp.start()
        sent.append(cp)
        return i

    def arrived(i, region):
        pltpu.make_async_remote_copy(
            src_ref=region, dst_ref=region, send_sem=ssem.at[i], recv_sem=rsem.at[i],
            device_id=sib, device_id_type=MESH,
        ).wait_recv()

    def gather_stages(buf):
        lo, hi = pl.ds(0, 64), pl.ds(64, 64)

        def own(ref):
            buf[k, y, x] = ref[...]

        def p1():
            a, b = buf.at[k, y, x, lo], buf.at[k, y, x, hi]
            return [start(a, a, xdev[1]), start(a, a, xdev[-1]), start(b, b, ydev[1]), start(b, b, ydev[-1])]

        def p1f(ids):
            arrived(ids[0], buf.at[k, y, xo(-1), lo])
            s = buf.at[k, y, xo(-1), pl.ds(0, 32)]
            out = [start(s, s, xdev[1])]
            arrived(ids[1], buf.at[k, y, xo(1), lo])
            s = buf.at[k, y, xo(1), pl.ds(32, 32)]
            out.append(start(s, s, xdev[-1]))
            arrived(ids[2], buf.at[k, yo(-1), x, hi])
            s = buf.at[k, yo(-1), x, pl.ds(64, 32)]
            out.append(start(s, s, ydev[1]))
            arrived(ids[3], buf.at[k, yo(1), x, hi])
            s = buf.at[k, yo(1), x, pl.ds(96, 32)]
            out.append(start(s, s, ydev[-1]))
            return out

        def p2(ids):
            arrived(ids[0], buf.at[k, y, xo(2), pl.ds(0, 32)])
            arrived(ids[1], buf.at[k, y, xo(2), pl.ds(32, 32)])
            a = buf.at[k, y, :, lo]
            out = [start(a, a, ydev[1]), start(a, a, ydev[-1])]
            arrived(ids[2], buf.at[k, yo(2), x, pl.ds(64, 32)])
            arrived(ids[3], buf.at[k, yo(2), x, pl.ds(96, 32)])
            b = buf.at[k, :, x, hi]
            return out + [start(b, b, xdev[1]), start(b, b, xdev[-1])]

        def p2f(ids):
            arrived(ids[0], buf.at[k, yo(-1), :, lo])
            s = buf.at[k, yo(-1), pl.ds(0, 2), lo]
            out = [start(s, s, ydev[1])]
            arrived(ids[1], buf.at[k, yo(1), :, lo])
            s = buf.at[k, yo(1), pl.ds(2, 2), lo]
            out.append(start(s, s, ydev[-1]))
            arrived(ids[2], buf.at[k, :, xo(-1), hi])
            s = buf.at[k, pl.ds(0, 2), xo(-1), hi]
            out.append(start(s, s, xdev[1]))
            arrived(ids[3], buf.at[k, :, xo(1), hi])
            s = buf.at[k, pl.ds(2, 2), xo(1), hi]
            out.append(start(s, s, xdev[-1]))
            return out

        def to_sib(ids):
            arrived(ids[0], buf.at[k, yo(2), pl.ds(0, 2), lo])
            arrived(ids[1], buf.at[k, yo(2), pl.ds(2, 2), lo])
            arrived(ids[2], buf.at[k, pl.ds(0, 2), xo(2), hi])
            arrived(ids[3], buf.at[k, pl.ds(2, 2), xo(2), hi])
            return [start(buf.at[k], buf.at[k], sib)]

        def done(ids):
            arrived(ids[0], buf.at[1 - k])

        return own, p1, p1f, p2, p2f, to_sib, done

    def ring_send(buf, h, d, s):
        piece = buf.at[h, zo(-SIGN[d] * (s - 1))]
        return start(piece, piece, zdev[SIGN[d]])

    def ring_wait(buf, ids, h, d, s):
        arrived(ids[h, d, s], buf.at[h, zo(-SIGN[d] * s)])

    def ring_step(buf, ids, s):
        for h in range(2):
            for d in range(2):
                if s <= ring_length(h, d):
                    ring_wait(buf, ids, h, d, s)
                    if s + 1 <= ring_length(h, d):
                        ids[h, d, s + 1] = ring_send(buf, h, d, s + 1)

    pl.semaphore_wait(barrier, len(everyone))

    g_own, g_p1, g_p1f, g_p2, g_p2f, g_sib, g_done = gather_stages(g_all)
    x_own, x_p1, x_p1f, x_p2, x_p2f, x_sib, x_done = gather_stages(x_all)

    g_own(g_ref)
    gi = g_p1()
    act_ids = {}
    for h in range(2):
        for q in range(2):
            j = q * 2 + h
            value, slope = gelu_parts(pre_ref[:, j * TB:(j + 1) * TB].astype(f32))
            act_all[h, z, :, q * TB:(q + 1) * TB] = value.astype(bf16)
            slope_s[h, :, q * TB:(q + 1) * TB] = slope
        for d in range(2):
            act_ids[h, d, 1] = ring_send(act_all, h, d, 1)
    gi = g_p1f(gi)
    x_own(x_ref)
    tr_s[...] = jnp.zeros_like(tr_s)
    tr_s[0:FB, :] = win_ref[...].astype(f32)
    for q in range(5):
        wt_s[q * TB:(q + 1) * TB, :] = jnp.transpose(tr_s[:, q * TB:(q + 1) * TB])[:, 0:FB].astype(bf16)
    gi = g_p2(gi)
    ring_step(act_all, act_ids, 1)
    gi = g_p2f(gi)
    gi = g_sib(gi)
    xi = x_p1()
    ring_step(act_all, act_ids, 2)
    xi = x_p1f(xi)
    xi = x_p2(xi)
    ring_step(act_all, act_ids, 3)
    g_done(gi)

    def tokens(buf, h, zz):
        return buf[h, zz // 2, pl.ds((zz % 2) * 2, 2)].reshape(2 * TB, DB)

    def partial_products(lo_i, hi_i):
        def body(i, _):
            h = i % 2
            q = i // 2
            o = 4 - (q % 2) * ((q + 1) // 2) + (1 - q % 2) * (q // 2)
            zz = (z + o) % 8
            hp[h, zz] = dot_nt(wout_ref[...], tokens(g_all, h, zz)).astype(bf16)
            return 0

        lax.fori_loop(lo_i, hi_i, body, 0)

    rs_ids = {}

    def rs_send(h, d, s):
        n = ring_length(h, d)
        dest = zo(SIGN[d] * (n - s + 1))
        if s == 1:
            src = hp.at[h, dest]
        else:
            src = rs_buf.at[h, d, s - 2]
            arrived(rs_ids[h, d, s - 1], src)
            rs_buf[h, d, s - 2] = (
                rs_buf[h, d, s - 2].astype(f32) + hp[h, dest].astype(f32)
            ).astype(bf16)
        rs_ids[h, d, s] = start(src, rs_buf.at[h, d, s - 1], zdev[SIGN[d]])

    def rs_step(s):
        for h in range(2):
            for d in range(2):
                if s <= ring_length(h, d):
                    rs_send(h, d, s)

    partial_products(0, 6)
    rs_step(1)
    partial_products(6, 16)
    xi = x_p2f(xi)
    rs_step(2)

    ring_step(act_all, act_ids, 4)

    def wgrad(acc, left, right, lo_i, hi_i):
        def body(i, _):
            acc[...] += dot_nn(left[0, i], tokens(right, 0, i)) + dot_nn(left[1, i], tokens(right, 1, i))
            return 0

        lax.fori_loop(lo_i, hi_i, body, 0)

    acc_out[...] = jnp.zeros_like(acc_out)
    wgrad(acc_out, act_all, g_all, 0, 4)
    rs_step(3)
    xi = x_sib(xi)
    wgrad(acc_out, act_all, g_all, 4, 8)
    rs_step(4)

    def square_sums(acc, off_row, off_col):
        total = jnp.zeros((FB, 1), f32)
        for q in range(5):
            c = slice(q * TB, (q + 1) * TB)
            v = acc[:, c]
            v = v * v
            col_st[0:1, off_col + q * TB:off_col + (q + 1) * TB] = jnp.sum(v, axis=0, keepdims=True)
            total += jnp.sum(v, axis=1, keepdims=True)
        tr_s[0:FB, 0:TB] = jnp.broadcast_to(total, (FB, TB))
        row_st[0:1, off_row:off_row + 512] = jnp.transpose(tr_s[:, 0:TB])[0:1, :]

    square_sums(acc_out, 512, 640)

    p_ids = {}
    for h in range(2):
        total = hp[h, z].astype(f32)
        for d in range(2):
            n = ring_length(h, d)
            arrived(rs_ids[h, d, n], rs_buf.at[h, d, n - 1])
            total += rs_buf[h, d, n - 1].astype(f32)
        p_all[h, z] = (total * slope_s[h]).astype(bf16)
        for d in range(2):
            p_ids[h, d, 1] = ring_send(p_all, h, d, 1)
    x_done(xi)

    acc_in[...] = jnp.zeros_like(acc_in)

    def sib_copy(h, zz):
        yy, x0 = zz // 2, (zz % 2) * 2
        return pltpu.make_async_remote_copy(
            src_ref=ipart.at[h, yy, pl.ds(x0, 2), pl.ds((1 - k) * HALF, HALF)],
            dst_ref=sib_buf.at[h, yy, pl.ds(x0, 2)],
            send_sem=sib_ss.at[h, zz], recv_sem=sib_rs.at[h, zz],
            device_id=sib, device_id_type=MESH,
        )

    def consume(h, zz):
        yy, x0 = zz // 2, (zz % 2) * 2
        pt = p_all[h, zz]
        part = dot_nn(wt_s[...], pt)
        ipart[h, yy, x0] = part[:, 0:TB].astype(bf16)
        ipart[h, yy, x0 + 1] = part[:, TB:2 * TB].astype(bf16)
        sib_copy(h, zz).start()
        acc_in[...] += dot_nn(pt, tokens(x_all, h, zz))

    def join(h, zz):
        yy, x0 = zz // 2, (zz % 2) * 2
        sib_copy(h, zz).wait_recv()
        rows = pl.ds(pl.multiple_of(k * HALF, HALF), HALF)
        for q in range(2):
            ipart[h, yy, x0 + q, rows, :] = (
                ipart[h, yy, x0 + q, rows, :].astype(f32) + sib_buf[h, yy, x0 + q].astype(f32)
            ).astype(bf16)

    def blocks(fn, s):
        if s == 0:
            def body(i, _):
                fn(i, z)
                return 0
            lax.fori_loop(0, 2, body, 0)
        elif s < 4:
            def body(i, _):
                h = i // 2
                fn(h, (z + 8 + (2 * (i % 2) - 1) * s) % 8)
                return 0
            lax.fori_loop(0, 4, body, 0)
        else:
            def body(i, _):
                fn(i, (z + 4) % 8)
                return 0
            lax.fori_loop(0, 2, body, 0)

    blocks(consume, 0)
    for s in range(1, 5):
        ring_step(p_all, p_ids, s)
        blocks(consume, s)
        blocks(join, s - 1)
    blocks(join, 4)

    base = pl.multiple_of(k * HALF, HALF)

    def feature_rows(off, size):
        return pl.ds(pl.multiple_of(base + off, 16), size)

    a_rows, b_rows = feature_rows(0, QUART), feature_rows(QUART, QUART)
    au, av = feature_rows(0, EIGHTH), feature_rows(EIGHTH, EIGHTH)
    bu, bv = feature_rows(QUART, EIGHTH), feature_rows(QUART + EIGHTH, EIGHTH)

    def add_to(view, *others):
        v = view[...].astype(f32)
        for o in others:
            v += o[...].astype(f32)
        view[...] = v.astype(bf16)

    def ring4(slab, off, devs, ru, rv, rp, rm, rows_all, rows_u, rows_v):
        def s1():
            return [
                start(slab(off(2), rows_u), ru, devs[1]),
                start(slab(off(2), rows_v), rv, devs[-1]),
            ]

        def s2(ids):
            arrived(ids[0], ru)
            add_to(slab(off(1), rows_u), ru)
            out = [start(slab(off(1), rows_all), rp, devs[1])]
            arrived(ids[1], rv)
            add_to(slab(off(-1), rows_v), rv)
            return out + [start(slab(off(-1), rows_all), rm, devs[-1])]

        def s3(ids):
            arrived(ids[0], rp)
            arrived(ids[1], rm)
            add_to(slab(off(0), rows_all), rp, rm)

        return s1, s2, s3

    ya = ring4(lambda o, rr: ipart.at[:, o, :, rr], yo, ydev, y_u, y_v, y_p, y_m, a_rows, au, av)
    xb = ring4(lambda o, rr: ipart.at[:, :, o, rr], xo, xdev, x_u, x_v, x_p, x_m, b_rows, bu, bv)
    xa = ring4(lambda o, rr: ipart.at[:, y, o, rr], xo, xdev, a2u, a2v, a2p, a2m, a_rows, au, av)
    yb = ring4(lambda o, rr: ipart.at[:, o, x, rr], yo, ydev, b2u, b2v, b2p, b2m, b_rows, bu, bv)

    i1, i2 = ya[0](), xb[0]()
    square_sums(acc_in, 0, 0)

    xk_slots = [xo(-(o // 2)) * 2 + (k + o) % 2 for o in range(1, 8)]
    y_slots = [yo(-o) for o in range(1, 4)]
    z_slots = [zo(-o) for o in range(1, 8)]

    def exchange(src, rx, me, peers):
        rx[me] = src[...]
        return [start(src, rx.at[me], p) for p in peers]

    def collect(ids, rx, slots, n):
        for i, slot in zip(ids, slots):
            arrived(i, rx.at[slot])
        total = rx[0]
        for j in range(1, n):
            total += rx[j]
        return total

    row_ids = exchange(row_st, row_rx, z, z_peers)
    col_ids = exchange(col_st, col_rx, x * 2 + k, xk_peers)
    i1, i2 = ya[1](i1), xb[1](i2)
    col2_st[...] = collect(col_ids, col_rx, xk_slots, 8)
    col_ids = exchange(col2_st, col2_rx, y, y_peers)
    row_sum = collect(row_ids, row_rx, z_slots, 8)
    prev_s[...] = jnp.ones_like(prev_s)
    prev_s[0:1, 0:FB] = rip_ref[...]
    prev_s[0:1, 512:512 + FB] = rop_ref[...]
    row_new = decay_rate * prev_s[...] + (1.0 - decay_rate) * (row_sum / D + epsilon_sq)
    ri_ref[...] = row_new[:, 0:FB]
    ro_ref[...] = row_new[:, 512:512 + FB]
    row_f = 1.0 / jnp.sqrt(row_new)
    ya[2](i1)
    xb[2](i2)
    i1, i2 = xa[0](), yb[0]()
    col_sum = collect(col_ids, col2_rx, y_slots, 4)
    col_in = decay_rate * cip_ref[...] + (1.0 - decay_rate) * (col_sum[:, 0:DB] / FF + epsilon_sq)
    col_out = decay_rate * cop_ref[...] + (1.0 - decay_rate) * (col_sum[:, DB:2 * DB] / FF + epsilon_sq)
    ci_ref[...] = col_in
    co_ref[...] = col_out
    root_tokens = math.sqrt(TOKENS)

    def raw_update(acc, out_ref, row_part, col, off):
        rows = jnp.transpose(jnp.broadcast_to(row_part, (TB, 512)))[0:FB, :]
        factor = root_tokens / jnp.sqrt(col)
        total = jnp.zeros((1, TB), f32)
        for q in range(5):
            c = slice(q * TB, (q + 1) * TB)
            v = acc[:, c] * (rows * factor[:, c])
            out_ref[:, c] = v
            total += jnp.sum(v * v, axis=0, keepdims=True)
        sc_st[0:1, off:off + TB] = total

    raw_update(acc_in, ui_ref, row_f[:, 0:512], col_in, 0)
    raw_update(acc_out, uo_ref, row_f[:, 512:1024], col_out, TB)
    sc_ids = exchange(sc_st, sc_rx1, x * 2 + k, xk_peers)
    i1, i2 = xa[1](i1), yb[1](i2)
    sc2_st[...] = collect(sc_ids, sc_rx1, xk_slots, 8)
    sc_ids = exchange(sc2_st, sc_rx2, y, y_peers)
    xa[2](i1)
    yb[2](i2)
    half = pl.ds(pl.multiple_of(k * HALF, HALF), HALF)
    fin = start(ipart.at[1 - k, y, x, half], fin_buf, sib)
    sc3_st[...] = collect(sc_ids, sc_rx2, y_slots, 4)
    sc_ids = exchange(sc3_st, sc_rx3, z, z_peers)
    out_s[half, :] = ipart[k, y, x, half, :].astype(f32)
    arrived(fin, fin_buf)
    other = pl.ds(pl.multiple_of((1 - k) * HALF, HALF), HALF)
    out_s[other, :] = fin_buf[...].astype(f32)
    for q in range(5):
        c = slice(q * TB, (q + 1) * TB)
        ig_ref[:, c] = jnp.transpose(out_s[c, :]).astype(bf16)
    sc = collect(sc_ids, sc_rx3, z_slots, 8)

    def clip(out_ref, part):
        total = jnp.sum(part, axis=1, keepdims=True)
        rms = jnp.sqrt(total / (FF * D))
        out_ref[...] = out_ref[...] * (1.0 / jnp.maximum(1.0, rms / clip_limit))

    clip(ui_ref, sc[:, 0:TB])
    clip(uo_ref, sc[:, TB:2 * TB])

    for cp in sent:
        cp.wait_send()

    def drain(i, _):
        sib_copy(i // 8, i % 8).wait_send()
        return 0

    lax.fori_loop(0, 16, drain, 0)


COPIES = 128


def per_device(
    inputs, grad_out, pre_act, w_in, w_out, row_in_prev, col_in_prev, row_out_prev, col_out_prev
):
    vmem = pl.BlockSpec(memory_space=pltpu.VMEM)

    def v(*shape, dtype=bf16):
        return pltpu.VMEM(shape, dtype)

    outs = pl.pallas_call(
        kernel,
        out_shape=(
            jax.ShapeDtypeStruct((TB, DB), bf16),
            jax.ShapeDtypeStruct((FB, DB), f32),
            jax.ShapeDtypeStruct((1, FB), f32),
            jax.ShapeDtypeStruct((1, DB), f32),
            jax.ShapeDtypeStruct((FB, DB), f32),
            jax.ShapeDtypeStruct((1, FB), f32),
            jax.ShapeDtypeStruct((1, DB), f32),
        ),
        in_specs=[vmem] * 9,
        out_specs=[vmem] * 7,
        scratch_shapes=[
            v(2, 4, 4, TB, DB), v(2, 4, 4, TB, DB),
            v(2, 8, FB, 256), v(2, 8, FB, 256),
            v(2, FB, 256, dtype=f32),
            v(2, 8, FB, 256),
            v(2, 2, 4, FB, 256),
            v(DB, FB), v(512, DB, dtype=f32),
            v(FB, DB, dtype=f32), v(FB, DB, dtype=f32),
            v(2, 4, 4, DB, TB), v(2, 4, 4, HALF, TB),
            v(2, 4, EIGHTH, TB), v(2, 4, EIGHTH, TB), v(2, 4, QUART, TB), v(2, 4, QUART, TB),
            v(2, 4, EIGHTH, TB), v(2, 4, EIGHTH, TB), v(2, 4, QUART, TB), v(2, 4, QUART, TB),
            v(2, EIGHTH, TB), v(2, EIGHTH, TB), v(2, QUART, TB), v(2, QUART, TB),
            v(2, EIGHTH, TB), v(2, EIGHTH, TB), v(2, QUART, TB), v(2, QUART, TB),
            v(HALF, TB), v(DB, TB, dtype=f32),
            v(1, 1024, dtype=f32), v(8, 1, 1024, dtype=f32), v(1, 1024, dtype=f32),
            v(1, 1280, dtype=f32), v(8, 1, 1280, dtype=f32),
            v(1, 1280, dtype=f32), v(4, 1, 1280, dtype=f32),
            v(1, 256, dtype=f32), v(1, 256, dtype=f32), v(1, 256, dtype=f32),
            v(8, 1, 256, dtype=f32), v(4, 1, 256, dtype=f32), v(8, 1, 256, dtype=f32),
            pltpu.SemaphoreType.DMA((COPIES,)), pltpu.SemaphoreType.DMA((COPIES,)),
            pltpu.SemaphoreType.DMA((2, 8)), pltpu.SemaphoreType.DMA((2, 8)),
        ],
        compiler_params=pltpu.CompilerParams(
            collective_id=0, has_side_effects=True, vmem_limit_bytes=60 * 1024 * 1024
        ),
        name="ffn_backward",
    )(
        inputs, grad_out, pre_act.T, w_in, w_out,
        row_in_prev[None], col_in_prev[None], row_out_prev[None], col_out_prev[None],
    )
    ig, ui, ri, ci, uo, ro, co = outs
    return ig, ui, ri[0], ci[0], uo, ro[0], co[0]


def solution(mesh):
    return jax.shard_map(
        per_device,
        mesh=mesh,
        in_specs=(
            P("row", "col"),
            P("row", "col"),
            P("col", "row"),
            P("row", "col"),
            P("row", "col"),
            P("row"),
            P("col"),
            P("row"),
            P("col"),
        ),
        out_specs=(
            P("row", "col"),
            P("row", "col"),
            P("row"),
            P("col"),
            P("row", "col"),
            P("row"),
            P("col"),
        ),
        check_vma=False,
    )
```

```python
import math

import jax
import jax.numpy as jnp
from jax import lax
from jax.experimental import pallas as pl
from jax.experimental.pallas import tpu as pltpu
from jax.sharding import PartitionSpec as P

D = 5120
FF = 13824
TOKENS = 4096
NY, NX, NK, NZ = 4, 4, 2, 8
TB = 128
FB = 432
DB = 640
HALF = DB // 2
QUART = DB // 4
EIGHTH = DB // 8

decay_rate = 0.8
epsilon_sq = 1e-30
clip_limit = 0.25
gelu_coef = 0.044715
root_coef = math.sqrt(2.0 / math.pi)

MESH = pl.DeviceIdType.MESH
bf16 = jnp.bfloat16
f32 = jnp.float32


def gelu_parts(p):
    t = jnp.tanh(root_coef * (p + gelu_coef * p * p * p))
    value = 0.5 * p * (1.0 + t)
    slope = 0.5 * (1.0 + t) + 0.5 * p * (1.0 - t * t) * root_coef * (
        1.0 + 3.0 * gelu_coef * p * p
    )
    return value, slope


def dot_nt(a, b):
    return lax.dot_general(a, b, (((1,), (1,)), ((), ())), preferred_element_type=f32)


def dot_nn(a, b):
    return lax.dot_general(a, b, (((1,), (0,)), ((), ())), preferred_element_type=f32)


def dot_tn(a, b):
    return lax.dot_general(a, b, (((0,), (0,)), ((), ())), preferred_element_type=f32)


def kernel(
    x_ref, g_ref, pre_ref, win_ref, wout_ref, rip_ref, cip_ref, rop_ref, cop_ref,
    ig_ref, ui_ref, uo_ref, rows_ref, cols_ref, sums_ref,
    g_all, x_all, act_all, p_all, slope_s, hp, rs_buf, pre_s, win_s, wout_s, tr_s,
    acc_out, acc_in, ipart, sib_buf, y_u, y_v, y_p, y_m, x_u, x_v, x_p, x_m,
    a2u, a2v, a2p, a2m, b2u, b2v, b2p, b2m, fin_buf, out_s, ig_s,
    rip_s, cip_s, rop_s, cop_s, rows_o, cols_o, sums_o,
    row_st, row_rx, col_st, col_rx, col2_st, col2_rx,
    sc_st, sc2_st, sc3_st, sc_rx1, sc_rx2, sc_rx3,
    ssem, rsem, sib_ss, sib_rs, act_ss, act_rs, p_ss, p_rs, h_ss, h_rs, io_sem,
):
    r = lax.axis_index("row")
    z = lax.axis_index("col")
    y = r // 8
    x = (r // 2) % 4
    k = r % 2

    def dev(yy, xx, kk, zz):
        return ((yy * 4 + xx) * 2 + kk, zz)

    def yo(o):
        return (y + (o + 4)) % 4

    def xo(o):
        return (x + (o + 4)) % 4

    def zo(o):
        return (z + (o + 8)) % 8

    sib = dev(y, x, 1 - k, z)
    xdev = {1: dev(y, xo(1), k, z), -1: dev(y, xo(-1), k, z)}
    ydev = {1: dev(yo(1), x, k, z), -1: dev(yo(-1), x, k, z)}
    xk_peers = [dev(y, xo(o // 2), (k + o) % 2, z) for o in range(1, 8)]
    y_peers = [dev(yo(o), x, k, z) for o in range(1, 4)]
    z_peers = [dev(y, x, k, zo(o)) for o in range(1, 8)]

    barrier = pltpu.get_barrier_semaphore()
    everyone = xk_peers + y_peers + z_peers
    for p in everyone:
        pl.semaphore_signal(barrier, inc=1, device_id=p, device_id_type=MESH)

    loads = {}
    for i, (name, src, dst) in enumerate((
        ("g", g_ref, g_all.at[k, y, x]),
        ("pre", pre_ref, pre_s),
        ("wout", wout_ref, wout_s),
        ("x", x_ref, x_all.at[k, y, x]),
        ("win", win_ref, win_s),
        ("rip", rip_ref, rip_s),
        ("rop", rop_ref, rop_s),
        ("cip", cip_ref, cip_s),
        ("cop", cop_ref, cop_s),
    )):
        loads[name] = pltpu.make_async_copy(src, dst, io_sem.at[i])
        loads[name].start()

    count = [0]
    sent = []

    def start(src, dst, peer):
        i = count[0]
        count[0] += 1
        cp = pltpu.make_async_remote_copy(
            src_ref=src, dst_ref=dst, send_sem=ssem.at[i], recv_sem=rsem.at[i],
            device_id=peer, device_id_type=MESH,
        )
        cp.start()
        sent.append(cp)
        return i

    def arrived(i, region):
        pltpu.make_async_remote_copy(
            src_ref=region, dst_ref=region, send_sem=ssem.at[i], recv_sem=rsem.at[i],
            device_id=sib, device_id_type=MESH,
        ).wait_recv()

    def gather_stages(buf):
        lo, hi = pl.ds(0, 64), pl.ds(64, 64)
        shared = []

        def share(view):
            shared.append((start(view(k), view(k), sib), view))

        def p1():
            a, b = buf.at[k, y, x, lo], buf.at[k, y, x, hi]
            return [start(a, a, xdev[1]), start(a, a, xdev[-1]), start(b, b, ydev[1]), start(b, b, ydev[-1])]

        def p1f(ids):
            arrived(ids[0], buf.at[k, y, xo(-1), lo])
            s = buf.at[k, y, xo(-1), pl.ds(0, 32)]
            out = [start(s, s, xdev[1])]
            arrived(ids[1], buf.at[k, y, xo(1), lo])
            s = buf.at[k, y, xo(1), pl.ds(32, 32)]
            out.append(start(s, s, xdev[-1]))
            arrived(ids[2], buf.at[k, yo(-1), x, hi])
            s = buf.at[k, yo(-1), x, pl.ds(64, 32)]
            out.append(start(s, s, ydev[1]))
            arrived(ids[3], buf.at[k, yo(1), x, hi])
            s = buf.at[k, yo(1), x, pl.ds(96, 32)]
            out.append(start(s, s, ydev[-1]))
            return out

        def p2(ids):
            arrived(ids[0], buf.at[k, y, xo(2), pl.ds(0, 32)])
            arrived(ids[1], buf.at[k, y, xo(2), pl.ds(32, 32)])
            a = buf.at[k, y, :, lo]
            out = [start(a, a, ydev[1]), start(a, a, ydev[-1])]
            arrived(ids[2], buf.at[k, yo(2), x, pl.ds(64, 32)])
            arrived(ids[3], buf.at[k, yo(2), x, pl.ds(96, 32)])
            b = buf.at[k, :, x, hi]
            out += [start(b, b, xdev[1]), start(b, b, xdev[-1])]
            share(lambda kk: buf.at[kk, y, :, lo])
            share(lambda kk: buf.at[kk, :, x, hi])
            return out

        def p2f(ids):
            arrived(ids[0], buf.at[k, yo(-1), :, lo])
            s = buf.at[k, yo(-1), pl.ds(0, 2), lo]
            out = [start(s, s, ydev[1])]
            arrived(ids[1], buf.at[k, yo(1), :, lo])
            s = buf.at[k, yo(1), pl.ds(2, 2), lo]
            out.append(start(s, s, ydev[-1]))
            arrived(ids[2], buf.at[k, :, xo(-1), hi])
            s = buf.at[k, pl.ds(0, 2), xo(-1), hi]
            out.append(start(s, s, xdev[1]))
            arrived(ids[3], buf.at[k, :, xo(1), hi])
            s = buf.at[k, pl.ds(2, 2), xo(1), hi]
            out.append(start(s, s, xdev[-1]))
            share(lambda kk: buf.at[kk, yo(-1), :, lo])
            share(lambda kk: buf.at[kk, yo(1), :, lo])
            share(lambda kk: buf.at[kk, :, xo(-1), hi])
            share(lambda kk: buf.at[kk, :, xo(1), hi])
            return out

        def last(ids):
            arrived(ids[0], buf.at[k, yo(2), pl.ds(0, 2), lo])
            arrived(ids[1], buf.at[k, yo(2), pl.ds(2, 2), lo])
            share(lambda kk: buf.at[kk, yo(2), :, lo])
            arrived(ids[2], buf.at[k, pl.ds(0, 2), xo(2), hi])
            arrived(ids[3], buf.at[k, pl.ds(2, 2), xo(2), hi])
            share(lambda kk: buf.at[kk, :, xo(2), hi])

        def done():
            for i, view in shared:
                arrived(i, view(1 - k))

        return p1, p1f, p2, p2f, last, done

    def stream(u):
        s = u // 4
        j = u % 4
        h = j % 2
        d = (j % 2 + j // 2) % 2
        return s, j, h, 1 - 2 * d

    def block(u):
        s, _, h, sign = stream(u)
        return h, (z + 8 - sign * s) % 8

    def ring_peer(sign):
        return (r, (z + 8 + sign) % 8)

    def ag_copy(buf, ss, rs, u):
        s, _, h, sign = stream(u)
        piece = buf.at[h, (z + 8 - sign * (s - 1)) % 8]
        return pltpu.make_async_remote_copy(
            src_ref=piece, dst_ref=piece, send_sem=ss.at[u], recv_sem=rs.at[u],
            device_id=ring_peer(sign), device_id_type=MESH,
        )

    def ag_wait(buf, ss, rs, u):
        h, zz = block(u)
        piece = buf.at[h, zz]
        pltpu.make_async_remote_copy(
            src_ref=piece, dst_ref=piece, send_sem=ss.at[u], recv_sem=rs.at[u],
            device_id=sib, device_id_type=MESH,
        ).wait_recv()

    act = (act_all, act_ss, act_rs)
    pg = (p_all, p_ss, p_rs)

    def act_pass(lo_u, hi_u):
        def body(u, _):
            ag_wait(*act, u)
            ag_copy(*act, u + 4).start()
            return 0

        lax.fori_loop(lo_u, hi_u, body, 0)

    g_p1, g_p1f, g_p2, g_p2f, g_last, g_done = gather_stages(g_all)
    x_p1, x_p1f, x_p2, x_p2f, x_last, x_done = gather_stages(x_all)

    loads["g"].wait()
    pl.semaphore_wait(barrier, len(everyone))
    gi = g_p1()
    loads["pre"].wait()
    for h in range(2):
        for q in range(2):
            j = q * 2 + h
            value, slope = gelu_parts(pre_s[:, j * TB:(j + 1) * TB].astype(f32))
            act_all[h, z, :, q * TB:(q + 1) * TB] = value.astype(bf16)
            slope_s[h, :, q * TB:(q + 1) * TB] = slope
        ag_copy(*act, 4 + h).start()
        ag_copy(*act, 6 + h).start()
    gi = g_p1f(gi)
    gi = g_p2(gi)
    act_pass(4, 8)
    gi = g_p2f(gi)
    loads["x"].wait()
    xi = x_p1()
    tr_s[...] = jnp.zeros_like(tr_s)
    act_pass(8, 10)
    g_last(gi)
    loads["wout"].wait()
    g_done()

    def tokens(buf, h, zz):
        return buf[h, zz // 2, pl.ds((zz % 2) * 2, 2)].reshape(2 * TB, DB)

    def partial_products(lo_i, hi_i):
        def body(i, _):
            h = i % 2
            q = i // 2
            o = 4 - (q % 2) * ((q + 1) // 2) + (1 - q % 2) * (q // 2)
            zz = (z + o) % 8
            hp[h, zz] = dot_nt(wout_s[...], tokens(g_all, h, zz)).astype(bf16)
            return 0

        lax.fori_loop(lo_i, hi_i, body, 0)

    def rs_dest(u):
        s, j, h, sign = stream(u)
        return h, (z + 8 + sign * (5 - j // 2 - s)) % 8, sign

    def rs_copy(src, u):
        _, _, sign = rs_dest(u)
        return pltpu.make_async_remote_copy(
            src_ref=src, dst_ref=rs_buf.at[u - 4], send_sem=h_ss.at[u], recv_sem=h_rs.at[u],
            device_id=ring_peer(sign), device_id_type=MESH,
        )

    def rs_first(u, _):
        h, dest, _ = rs_dest(u)
        rs_copy(hp.at[h, dest], u).start()
        return 0

    def rs_wait(u):
        rs_copy(rs_buf.at[u - 4], u).wait_recv()

    def wgrad_block(acc, left, right, u):
        h, zz = block(u)
        acc[...] += dot_nn(left[h, zz], tokens(right, h, zz))

    def rs_next(u, _):
        h, dest, _ = rs_dest(u)
        rs_wait(u - 4)
        rs_buf[u - 8] = (rs_buf[u - 8].astype(f32) + hp[h, dest].astype(f32)).astype(bf16)
        rs_copy(rs_buf.at[u - 8], u).start()

        @pl.when(u < 16)
        def _():
            wgrad_block(acc_out, act_all, g_all, u - 6)

        return 0

    partial_products(0, 6)
    lax.fori_loop(4, 8, rs_first, 0)
    xi = x_p1f(xi)
    xi = x_p2(xi)
    partial_products(6, 16)
    acc_out[...] = jnp.zeros_like(acc_out)
    acc_in[...] = jnp.zeros_like(acc_in)
    lax.fori_loop(8, 12, rs_next, 0)
    xi = x_p2f(xi)
    lax.fori_loop(12, 18, rs_next, 0)
    x_last(xi)

    for h in range(2):
        total = hp[h, z].astype(f32)
        for u in (14 + h, 16 + h):
            rs_wait(u)
            total += rs_buf[u - 4].astype(f32)
        p_all[h, z] = (total * slope_s[h]).astype(bf16)
        ag_copy(*pg, 4 + h).start()
        ag_copy(*pg, 6 + h).start()
    loads["win"].wait()
    x_done()

    base = pl.multiple_of(k * HALF, HALF)
    half = pl.ds(base, HALF)
    other = pl.ds(pl.multiple_of((1 - k) * HALF, HALF), HALF)

    def sib_copy(h, zz):
        yy, x0 = zz // 2, (zz % 2) * 2
        return pltpu.make_async_remote_copy(
            src_ref=ipart.at[h, yy, pl.ds(x0, 2), other],
            dst_ref=sib_buf.at[h, yy, pl.ds(x0, 2)],
            send_sem=sib_ss.at[h, zz], recv_sem=sib_rs.at[h, zz],
            device_id=sib, device_id_type=MESH,
        )

    def consume(u):
        h, zz = block(u)
        yy, x0 = zz // 2, (zz % 2) * 2
        pt = p_all[h, zz]
        part = dot_tn(win_s[...], pt)
        ipart[h, yy, x0] = part[:, 0:TB].astype(bf16)
        ipart[h, yy, x0 + 1] = part[:, TB:2 * TB].astype(bf16)
        sib_copy(h, zz).start()
        acc_in[...] += dot_nn(pt, tokens(x_all, h, zz))

    def join(u):
        h, zz = block(u)
        yy, x0 = zz // 2, (zz % 2) * 2
        sib_copy(h, zz).wait_recv()
        for q in range(2):
            ipart[h, yy, x0 + q, half, :] = (
                ipart[h, yy, x0 + q, half, :].astype(f32) + sib_buf[h, yy, x0 + q].astype(f32)
            ).astype(bf16)

    def p_step(u, _):
        @pl.when(u >= 4)
        def _():
            ag_wait(*pg, u)

        @pl.when((u >= 4) & (u < 14))
        def _():
            ag_copy(*pg, u + 4).start()

        @pl.when(u >= 14)
        def _():
            ag_wait(*act, u - 4)
            ag_copy(*act, u).start()

        consume(u)

        @pl.when(u >= 5)
        def _():
            join(u - 3)

        return 0

    lax.fori_loop(2, 18, p_step, 0)

    def join_step(u, _):
        join(u)
        return 0

    lax.fori_loop(15, 18, join_step, 0)

    def feature_rows(off, size):
        return pl.ds(pl.multiple_of(base + off, 16), size)

    a_rows, b_rows = feature_rows(0, QUART), feature_rows(QUART, QUART)
    au, av = feature_rows(0, EIGHTH), feature_rows(EIGHTH, EIGHTH)
    bu, bv = feature_rows(QUART, EIGHTH), feature_rows(QUART + EIGHTH, EIGHTH)

    def add_to(view, *others):
        v = view[...].astype(f32)
        for o in others:
            v += o[...].astype(f32)
        view[...] = v.astype(bf16)

    def ring4(slab, off, devs, ru, rv, rp, rm, rows_all, rows_u, rows_v):
        def s1():
            return [
                start(slab(off(2), rows_u), ru, devs[1]),
                start(slab(off(2), rows_v), rv, devs[-1]),
            ]

        def s2(ids):
            arrived(ids[0], ru)
            add_to(slab(off(1), rows_u), ru)
            out = [start(slab(off(1), rows_all), rp, devs[1])]
            arrived(ids[1], rv)
            add_to(slab(off(-1), rows_v), rv)
            return out + [start(slab(off(-1), rows_all), rm, devs[-1])]

        def s3(ids):
            arrived(ids[0], rp)
            arrived(ids[1], rm)
            add_to(slab(off(0), rows_all), rp, rm)

        return s1, s2, s3

    ya = ring4(lambda o, rr: ipart.at[:, o, :, rr], yo, ydev, y_u, y_v, y_p, y_m, a_rows, au, av)
    xb = ring4(lambda o, rr: ipart.at[:, :, o, rr], xo, xdev, x_u, x_v, x_p, x_m, b_rows, bu, bv)
    xa = ring4(lambda o, rr: ipart.at[:, y, o, rr], xo, xdev, a2u, a2v, a2p, a2m, a_rows, au, av)
    yb = ring4(lambda o, rr: ipart.at[:, o, x, rr], yo, ydev, b2u, b2v, b2p, b2m, b_rows, bu, bv)

    i1, i2 = ya[0](), xb[0]()

    def square_sums(acc, off_row, off_col):
        total = jnp.zeros((FB, 1), f32)
        for q in range(5):
            c = slice(q * TB, (q + 1) * TB)
            v = acc[:, c]
            v = v * v
            col_st[0:1, off_col + q * TB:off_col + (q + 1) * TB] = jnp.sum(v, axis=0, keepdims=True)
            total += jnp.sum(v, axis=1, keepdims=True)
        tr_s[0:FB, :] = jnp.broadcast_to(total, (FB, TB))
        row_st[0:1, off_row:off_row + 512] = jnp.transpose(tr_s[...])[0:1, :]

    def wgrad_step(u, _):
        wgrad_block(acc_out, act_all, g_all, u)
        return 0

    lax.fori_loop(10, 14, wgrad_step, 0)
    square_sums(acc_in, 0, 0)
    i1, i2 = ya[1](i1), xb[1](i2)

    def act_last(u, _):
        ag_wait(*act, u)
        wgrad_block(acc_out, act_all, g_all, u)
        return 0

    lax.fori_loop(14, 18, act_last, 0)
    square_sums(acc_out, 512, 640)

    xk_slots = [xo(-(o // 2)) * 2 + (k + o) % 2 for o in range(1, 8)]
    y_slots = [yo(-o) for o in range(1, 4)]
    z_slots = [zo(-o) for o in range(1, 8)]

    def exchange(src, rx, me, peers):
        rx[me] = src[...]
        return [start(src, rx.at[me], p) for p in peers]

    def collect(ids, rx, slots, n):
        for i, slot in zip(ids, slots):
            arrived(i, rx.at[slot])
        total = rx[0]
        for j in range(1, n):
            total += rx[j]
        return total

    col_ids = exchange(col_st, col_rx, x * 2 + k, xk_peers)
    row_ids = exchange(row_st, row_rx, z, z_peers)
    ya[2](i1)
    xb[2](i2)
    i1, i2 = xa[0](), yb[0]()
    for name in ("rip", "rop", "cip", "cop"):
        loads[name].wait()
    col2_st[...] = collect(col_ids, col_rx, xk_slots, 8)
    col_ids = exchange(col2_st, col2_rx, y, y_peers)
    i1, i2 = xa[1](i1), yb[1](i2)
    row_sum = collect(row_ids, row_rx, z_slots, 8)

    def moment(prev, part, n):
        prev = prev[...].reshape(1, prev.shape[0])
        return decay_rate * prev + (1.0 - decay_rate) * (part / n + epsilon_sq)

    rows_o[...] = jnp.ones_like(rows_o)
    rows_o[0:1, 0:FB] = moment(rip_s, row_sum[:, 0:FB], D)
    rows_o[0:1, 512:512 + FB] = moment(rop_s, row_sum[:, 512:512 + FB], D)
    row_f = 1.0 / jnp.sqrt(rows_o[...])
    col_sum = collect(col_ids, col2_rx, y_slots, 4)
    cols_o[0:1, 0:DB] = moment(cip_s, col_sum[:, 0:DB], FF)
    cols_o[0:1, DB:2 * DB] = moment(cop_s, col_sum[:, DB:2 * DB], FF)
    root_tokens = math.sqrt(TOKENS)

    stores = []

    def store(src, dst):
        cp = pltpu.make_async_copy(src, dst, io_sem.at[9 + len(stores)])
        cp.start()
        stores.append(cp)

    store(rows_o, rows_ref)
    store(cols_o, cols_ref)

    def raw_update(acc, out_ref, row_part, col, off):
        rows = jnp.transpose(jnp.broadcast_to(row_part, (TB, 512)))[0:FB, :]
        factor = root_tokens / jnp.sqrt(col)
        total = jnp.zeros((1, TB), f32)
        for q in range(5):
            c = slice(q * TB, (q + 1) * TB)
            v = acc[:, c] * (rows * factor[:, c])
            acc[:, c] = v
            total += jnp.sum(v * v, axis=0, keepdims=True)
        sc_st[0:1, off:off + TB] = total
        store(acc, out_ref)

    raw_update(acc_in, ui_ref, row_f[:, 0:512], cols_o[0:1, 0:DB], 0)
    raw_update(acc_out, uo_ref, row_f[:, 512:1024], cols_o[0:1, DB:2 * DB], TB)
    sc_ids = exchange(sc_st, sc_rx1, x * 2 + k, xk_peers)
    xa[2](i1)
    yb[2](i2)
    fin = start(ipart.at[1 - k, y, x, half], fin_buf, sib)
    sc2_st[...] = collect(sc_ids, sc_rx1, xk_slots, 8)
    sc_ids = exchange(sc2_st, sc_rx2, y, y_peers)
    out_s[half, :] = ipart[k, y, x, half, :].astype(f32)
    arrived(fin, fin_buf)
    out_s[other, :] = fin_buf[...].astype(f32)
    for q in range(5):
        c = slice(q * TB, (q + 1) * TB)
        ig_s[:, c] = jnp.transpose(out_s[c, :]).astype(bf16)
    store(ig_s, ig_ref)
    sc3_st[...] = collect(sc_ids, sc_rx2, y_slots, 4)
    sc_ids = exchange(sc3_st, sc_rx3, z, z_peers)
    for cp in sent[:-len(z_peers)]:
        cp.wait_send()

    def drain(u, _):
        ag_copy(*act, u).wait_send()
        ag_copy(*pg, u).wait_send()
        rs_copy(rs_buf.at[u - 4], u).wait_send()
        return 0

    lax.fori_loop(4, 18, drain, 0)

    def sib_drain(i, _):
        sib_copy(i // 8, i % 8).wait_send()
        return 0

    lax.fori_loop(0, 16, sib_drain, 0)
    sums_o[...] = collect(sc_ids, sc_rx3, z_slots, 8)
    store(sums_o, sums_ref)
    for cp in sent[-len(z_peers):]:
        cp.wait_send()
    for cp in stores:
        cp.wait()


def finish(
    ig_in, ui_in, uo_in, rows, cols, sums,
    ig_ref, ui_ref, ri_ref, ci_ref, uo_ref, ro_ref, co_ref,
):
    ig_ref[...] = ig_in[...]

    def clip(raw, out_ref, part):
        total = jnp.sum(part, axis=1, keepdims=True)
        rms = jnp.sqrt(total / (FF * D))
        out_ref[...] = raw[...] * (1.0 / jnp.maximum(1.0, rms / clip_limit))

    clip(ui_in, ui_ref, sums[0:1, 0:TB])
    clip(uo_in, uo_ref, sums[0:1, TB:2 * TB])
    ri_ref[...] = rows[0:1, 0:FB].reshape(FB)
    ro_ref[...] = rows[0:1, 512:512 + FB].reshape(FB)
    ci_ref[...] = cols[0:1, 0:DB].reshape(DB)
    co_ref[...] = cols[0:1, DB:2 * DB].reshape(DB)


COPIES = 128


def per_device(
    inputs, grad_out, pre_act, w_in, w_out, row_in_prev, col_in_prev, row_out_prev, col_out_prev
):
    hbm = pl.BlockSpec(memory_space=pl.ANY)
    vmem = pl.BlockSpec(memory_space=pltpu.VMEM)
    dma = pltpu.SemaphoreType.DMA

    def v(*shape, dtype=bf16):
        return pltpu.VMEM(shape, dtype)

    ig, ui, uo, rows, cols, sums = pl.pallas_call(
        kernel,
        out_shape=(
            jax.ShapeDtypeStruct((TB, DB), bf16),
            jax.ShapeDtypeStruct((FB, DB), f32),
            jax.ShapeDtypeStruct((FB, DB), f32),
            jax.ShapeDtypeStruct((1, 1024), f32),
            jax.ShapeDtypeStruct((1, 1280), f32),
            jax.ShapeDtypeStruct((1, 256), f32),
        ),
        in_specs=[hbm] * 9,
        out_specs=[hbm] * 6,
        scratch_shapes=[
            v(2, 4, 4, TB, DB), v(2, 4, 4, TB, DB),
            v(2, 8, FB, 256), v(2, 8, FB, 256),
            v(2, FB, 256, dtype=f32),
            v(2, 8, FB, 256),
            v(14, FB, 256),
            v(FB, 512), v(FB, DB), v(FB, DB),
            v(512, TB, dtype=f32),
            v(FB, DB, dtype=f32), v(FB, DB, dtype=f32),
            v(2, 4, 4, DB, TB), v(2, 4, 4, HALF, TB),
            v(2, 4, EIGHTH, TB), v(2, 4, EIGHTH, TB), v(2, 4, QUART, TB), v(2, 4, QUART, TB),
            v(2, 4, EIGHTH, TB), v(2, 4, EIGHTH, TB), v(2, 4, QUART, TB), v(2, 4, QUART, TB),
            v(2, EIGHTH, TB), v(2, EIGHTH, TB), v(2, QUART, TB), v(2, QUART, TB),
            v(2, EIGHTH, TB), v(2, EIGHTH, TB), v(2, QUART, TB), v(2, QUART, TB),
            v(HALF, TB), v(DB, TB, dtype=f32), v(TB, DB),
            v(FB, dtype=f32), v(DB, dtype=f32), v(FB, dtype=f32), v(DB, dtype=f32),
            v(1, 1024, dtype=f32), v(1, 1280, dtype=f32), v(1, 256, dtype=f32),
            v(1, 1024, dtype=f32), v(8, 1, 1024, dtype=f32),
            v(1, 1280, dtype=f32), v(8, 1, 1280, dtype=f32),
            v(1, 1280, dtype=f32), v(4, 1, 1280, dtype=f32),
            v(1, 256, dtype=f32), v(1, 256, dtype=f32), v(1, 256, dtype=f32),
            v(8, 1, 256, dtype=f32), v(4, 1, 256, dtype=f32), v(8, 1, 256, dtype=f32),
            dma((COPIES,)), dma((COPIES,)), dma((2, 8)), dma((2, 8)),
            dma((18,)), dma((18,)), dma((18,)), dma((18,)), dma((18,)), dma((18,)), dma((16,)),
        ],
        compiler_params=pltpu.CompilerParams(
            collective_id=0, has_side_effects=True, vmem_limit_bytes=60 * 1024 * 1024
        ),
        name="ffn_backward",
    )(
        inputs, grad_out, pre_act.T, w_in, w_out,
        row_in_prev, col_in_prev, row_out_prev, col_out_prev,
    )
    return pl.pallas_call(
        finish,
        out_shape=(
            jax.ShapeDtypeStruct((TB, DB), bf16),
            jax.ShapeDtypeStruct((FB, DB), f32),
            jax.ShapeDtypeStruct((FB,), f32),
            jax.ShapeDtypeStruct((DB,), f32),
            jax.ShapeDtypeStruct((FB, DB), f32),
            jax.ShapeDtypeStruct((FB,), f32),
            jax.ShapeDtypeStruct((DB,), f32),
        ),
        in_specs=[vmem] * 6,
        out_specs=[vmem] * 7,
        compiler_params=pltpu.CompilerParams(vmem_limit_bytes=60 * 1024 * 1024),
        name="clip_updates",
    )(ig, ui, uo, rows, cols, sums)


def solution(mesh):
    return jax.shard_map(
        per_device,
        mesh=mesh,
        in_specs=(
            P("row", "col"),
            P("row", "col"),
            P("col", "row"),
            P("row", "col"),
            P("row", "col"),
            P("row"),
            P("col"),
            P("row"),
            P("col"),
        ),
        out_specs=(
            P("row", "col"),
            P("row", "col"),
            P("row"),
            P("col"),
            P("row", "col"),
            P("row"),
            P("col"),
        ),
        check_vma=False,
    )
```

```python
import math

import jax
import jax.numpy as jnp
from jax import lax
from jax.experimental import pallas as pl
from jax.experimental.pallas import tpu as pltpu
from jax.sharding import PartitionSpec as P

D = 5120
FF = 13824
TOKENS = 4096
NY, NX, NK, NZ = 4, 4, 2, 8
TB = 128
FB = 432
DB = 640
HALF = DB // 2
QUART = DB // 4
EIGHTH = DB // 8

decay_rate = 0.8
epsilon_sq = 1e-30
clip_limit = 0.25
gelu_coef = 0.044715
root_coef = math.sqrt(2.0 / math.pi)

MESH = pl.DeviceIdType.MESH
bf16 = jnp.bfloat16
f32 = jnp.float32


def gelu_parts(p):
    t = jnp.tanh(root_coef * (p + gelu_coef * p * p * p))
    value = 0.5 * p * (1.0 + t)
    slope = 0.5 * (1.0 + t) + 0.5 * p * (1.0 - t * t) * root_coef * (
        1.0 + 3.0 * gelu_coef * p * p
    )
    return value, slope


def dot_nt(a, b):
    return lax.dot_general(a, b, (((1,), (1,)), ((), ())), preferred_element_type=f32)


def dot_nn(a, b):
    return lax.dot_general(a, b, (((1,), (0,)), ((), ())), preferred_element_type=f32)


def dot_tn(a, b):
    return lax.dot_general(a, b, (((0,), (0,)), ((), ())), preferred_element_type=f32)


def kernel(
    x_ref, g_ref, pre_ref, win_ref, wout_ref, rip_ref, cip_ref, rop_ref, cop_ref,
    ig_ref, ui_ref, uo_ref, rows_ref, cols_ref, sums_ref,
    g_all, x_all, act_all, p_all, slope_s, hp, rs_buf, pre_s, win_s, wout_s, tr_s,
    acc_out, acc_in, ipart, sib_buf, y_u, y_v, y_p, y_m, x_u, x_v, x_p, x_m,
    a2u, a2v, a2p, a2m, b2u, b2v, b2p, b2m, fin_buf, out_s, ig_s,
    rip_s, cip_s, rop_s, cop_s, rows_o, cols_o, sums_o,
    row_st, row_rx, col_st, col_rx, col2_st, col2_rx,
    sc_st, sc2_st, sc3_st, sc_rx1, sc_rx2, sc_rx3,
    ssem, rsem, sib_ss, sib_rs, act_ss, act_rs, p_ss, p_rs, h_ss, h_rs, io_sem,
):
    r = lax.axis_index("row")
    z = lax.axis_index("col")
    y = r // 8
    x = (r // 2) % 4
    k = r % 2

    def dev(yy, xx, kk, zz):
        return ((yy * 4 + xx) * 2 + kk, zz)

    def yo(o):
        return (y + (o + 4)) % 4

    def xo(o):
        return (x + (o + 4)) % 4

    def zo(o):
        return (z + (o + 8)) % 8

    sib = dev(y, x, 1 - k, z)
    xdev = {1: dev(y, xo(1), k, z), -1: dev(y, xo(-1), k, z)}
    ydev = {1: dev(yo(1), x, k, z), -1: dev(yo(-1), x, k, z)}
    xk_peers = [dev(y, xo(o // 2), (k + o) % 2, z) for o in range(1, 8)]
    y_peers = [dev(yo(o), x, k, z) for o in range(1, 4)]
    z_peers = [dev(y, x, k, zo(o)) for o in range(1, 8)]

    barrier = pltpu.get_barrier_semaphore()
    everyone = xk_peers + y_peers + z_peers
    for p in everyone:
        pl.semaphore_signal(barrier, inc=1, device_id=p, device_id_type=MESH)

    loads = {}
    for i, (name, src, dst) in enumerate((
        ("g", g_ref, g_all.at[k, y, x]),
        ("pre", pre_ref, pre_s),
        ("wout", wout_ref, wout_s),
        ("x", x_ref, x_all.at[k, y, x]),
        ("win", win_ref, win_s),
        ("rip", rip_ref, rip_s),
        ("rop", rop_ref, rop_s),
        ("cip", cip_ref, cip_s),
        ("cop", cop_ref, cop_s),
    )):
        loads[name] = pltpu.make_async_copy(src, dst, io_sem.at[i])
        loads[name].start()

    count = [0]
    sent = []

    def start(src, dst, peer):
        i = count[0]
        count[0] += 1
        cp = pltpu.make_async_remote_copy(
            src_ref=src, dst_ref=dst, send_sem=ssem.at[i], recv_sem=rsem.at[i],
            device_id=peer, device_id_type=MESH,
        )
        cp.start()
        sent.append(cp)
        return i

    def arrived(i, region):
        pltpu.make_async_remote_copy(
            src_ref=region, dst_ref=region, send_sem=ssem.at[i], recv_sem=rsem.at[i],
            device_id=sib, device_id_type=MESH,
        ).wait_recv()

    def gather_stages(buf):
        lo, hi = pl.ds(0, 64), pl.ds(64, 64)
        shared = []

        def share(view):
            shared.append((start(view(k), view(k), sib), view))

        def p1():
            a, b = buf.at[k, y, x, lo], buf.at[k, y, x, hi]
            return [start(a, a, xdev[1]), start(a, a, xdev[-1]), start(b, b, ydev[1]), start(b, b, ydev[-1])]

        def p1f(ids):
            arrived(ids[0], buf.at[k, y, xo(-1), lo])
            s = buf.at[k, y, xo(-1), pl.ds(0, 32)]
            out = [start(s, s, xdev[1])]
            arrived(ids[1], buf.at[k, y, xo(1), lo])
            s = buf.at[k, y, xo(1), pl.ds(32, 32)]
            out.append(start(s, s, xdev[-1]))
            arrived(ids[2], buf.at[k, yo(-1), x, hi])
            s = buf.at[k, yo(-1), x, pl.ds(64, 32)]
            out.append(start(s, s, ydev[1]))
            arrived(ids[3], buf.at[k, yo(1), x, hi])
            s = buf.at[k, yo(1), x, pl.ds(96, 32)]
            out.append(start(s, s, ydev[-1]))
            return out

        def p2(ids):
            arrived(ids[0], buf.at[k, y, xo(2), pl.ds(0, 32)])
            arrived(ids[1], buf.at[k, y, xo(2), pl.ds(32, 32)])
            a = buf.at[k, y, :, lo]
            out = [start(a, a, ydev[1]), start(a, a, ydev[-1])]
            arrived(ids[2], buf.at[k, yo(2), x, pl.ds(64, 32)])
            arrived(ids[3], buf.at[k, yo(2), x, pl.ds(96, 32)])
            b = buf.at[k, :, x, hi]
            out += [start(b, b, xdev[1]), start(b, b, xdev[-1])]
            share(lambda kk: buf.at[kk, y, :, lo])
            share(lambda kk: buf.at[kk, :, x, hi])
            return out

        def p2f(ids):
            arrived(ids[0], buf.at[k, yo(-1), :, lo])
            s = buf.at[k, yo(-1), pl.ds(0, 2), lo]
            out = [start(s, s, ydev[1])]
            arrived(ids[1], buf.at[k, yo(1), :, lo])
            s = buf.at[k, yo(1), pl.ds(2, 2), lo]
            out.append(start(s, s, ydev[-1]))
            arrived(ids[2], buf.at[k, :, xo(-1), hi])
            s = buf.at[k, pl.ds(0, 2), xo(-1), hi]
            out.append(start(s, s, xdev[1]))
            arrived(ids[3], buf.at[k, :, xo(1), hi])
            s = buf.at[k, pl.ds(2, 2), xo(1), hi]
            out.append(start(s, s, xdev[-1]))
            share(lambda kk: buf.at[kk, yo(-1), :, lo])
            share(lambda kk: buf.at[kk, yo(1), :, lo])
            share(lambda kk: buf.at[kk, :, xo(-1), hi])
            share(lambda kk: buf.at[kk, :, xo(1), hi])
            return out

        def last(ids):
            arrived(ids[0], buf.at[k, yo(2), pl.ds(0, 2), lo])
            arrived(ids[1], buf.at[k, yo(2), pl.ds(2, 2), lo])
            share(lambda kk: buf.at[kk, yo(2), :, lo])
            arrived(ids[2], buf.at[k, pl.ds(0, 2), xo(2), hi])
            arrived(ids[3], buf.at[k, pl.ds(2, 2), xo(2), hi])
            share(lambda kk: buf.at[kk, :, xo(2), hi])

        def done():
            for i, view in shared:
                arrived(i, view(1 - k))

        return p1, p1f, p2, p2f, last, done

    def stream(u):
        s = u // 4
        j = u % 4
        h = j % 2
        d = (j % 2 + j // 2) % 2
        return s, j, h, 1 - 2 * d

    def block(u):
        s, _, h, sign = stream(u)
        return h, (z + 8 - sign * s) % 8

    def ring_peer(sign):
        return (r, (z + 8 + sign) % 8)

    def ag_copy(buf, ss, rs, u):
        s, _, h, sign = stream(u)
        piece = buf.at[h, (z + 8 - sign * (s - 1)) % 8]
        return pltpu.make_async_remote_copy(
            src_ref=piece, dst_ref=piece, send_sem=ss.at[u], recv_sem=rs.at[u],
            device_id=ring_peer(sign), device_id_type=MESH,
        )

    def ag_wait(buf, ss, rs, u):
        h, zz = block(u)
        piece = buf.at[h, zz]
        pltpu.make_async_remote_copy(
            src_ref=piece, dst_ref=piece, send_sem=ss.at[u], recv_sem=rs.at[u],
            device_id=sib, device_id_type=MESH,
        ).wait_recv()

    act = (act_all, act_ss, act_rs)
    pg = (p_all, p_ss, p_rs)

    def act_pass(lo_u, hi_u):
        def body(u, _):
            ag_wait(*act, u)
            ag_copy(*act, u + 4).start()
            return 0

        lax.fori_loop(lo_u, hi_u, body, 0)

    g_p1, g_p1f, g_p2, g_p2f, g_last, g_done = gather_stages(g_all)
    x_p1, x_p1f, x_p2, x_p2f, x_last, x_done = gather_stages(x_all)

    loads["g"].wait()
    pl.semaphore_wait(barrier, len(everyone))
    gi = g_p1()
    loads["pre"].wait()
    for h in range(2):
        for q in range(2):
            j = q * 2 + h
            value, slope = gelu_parts(pre_s[:, j * TB:(j + 1) * TB].astype(f32))
            act_all[h, z, :, q * TB:(q + 1) * TB] = value.astype(bf16)
            slope_s[h, :, q * TB:(q + 1) * TB] = slope
        ag_copy(*act, 4 + h).start()
    gi = g_p1f(gi)
    ag_copy(*act, 6).start()
    ag_copy(*act, 7).start()
    gi = g_p2(gi)
    act_pass(4, 8)
    gi = g_p2f(gi)
    loads["x"].wait()
    xi = x_p1()
    tr_s[...] = jnp.zeros_like(tr_s)
    act_pass(8, 10)
    g_last(gi)
    loads["wout"].wait()
    g_done()

    def tokens(buf, h, zz):
        return buf[h, zz // 2, pl.ds((zz % 2) * 2, 2)].reshape(2 * TB, DB)

    def partial_products(lo_i, hi_i):
        def body(i, _):
            h = i % 2
            q = i // 2
            o = 4 - (q % 2) * ((q + 1) // 2) + (1 - q % 2) * (q // 2)
            zz = (z + o) % 8
            hp[h, zz] = dot_nt(wout_s[...], tokens(g_all, h, zz)).astype(bf16)
            return 0

        lax.fori_loop(lo_i, hi_i, body, 0)

    def rs_dest(u):
        s, j, h, sign = stream(u)
        return h, (z + 8 + sign * (5 - j // 2 - s)) % 8, sign

    def rs_copy(src, u):
        _, _, sign = rs_dest(u)
        return pltpu.make_async_remote_copy(
            src_ref=src, dst_ref=rs_buf.at[u - 4], send_sem=h_ss.at[u], recv_sem=h_rs.at[u],
            device_id=ring_peer(sign), device_id_type=MESH,
        )

    def rs_first(u, _):
        h, dest, _ = rs_dest(u)
        rs_copy(hp.at[h, dest], u).start()
        return 0

    def rs_wait(u):
        rs_copy(rs_buf.at[u - 4], u).wait_recv()

    def wgrad_block(acc, left, right, u):
        h, zz = block(u)
        acc[...] += dot_nn(left[h, zz], tokens(right, h, zz))

    def rs_next(u, _):
        h, dest, _ = rs_dest(u)
        rs_wait(u - 4)
        rs_buf[u - 8] = (rs_buf[u - 8].astype(f32) + hp[h, dest].astype(f32)).astype(bf16)
        rs_copy(rs_buf.at[u - 8], u).start()

        @pl.when(u < 16)
        def _():
            wgrad_block(acc_out, act_all, g_all, u - 6)

        return 0

    partial_products(0, 2)
    lax.fori_loop(4, 6, rs_first, 0)
    partial_products(2, 6)
    lax.fori_loop(6, 8, rs_first, 0)
    xi = x_p1f(xi)
    xi = x_p2(xi)
    partial_products(6, 16)
    acc_out[...] = jnp.zeros_like(acc_out)
    acc_in[...] = jnp.zeros_like(acc_in)
    lax.fori_loop(8, 12, rs_next, 0)
    xi = x_p2f(xi)
    lax.fori_loop(12, 18, rs_next, 0)
    x_last(xi)

    for h in range(2):
        total = hp[h, z].astype(f32)
        for u in (14 + h, 16 + h):
            rs_wait(u)
            total += rs_buf[u - 4].astype(f32)
        p_all[h, z] = (total * slope_s[h]).astype(bf16)
        ag_copy(*pg, 4 + h).start()
    loads["win"].wait()
    x_done()

    base = pl.multiple_of(k * HALF, HALF)
    half = pl.ds(base, HALF)
    other = pl.ds(pl.multiple_of((1 - k) * HALF, HALF), HALF)

    def sib_copy(h, zz):
        yy, x0 = zz // 2, (zz % 2) * 2
        return pltpu.make_async_remote_copy(
            src_ref=ipart.at[h, yy, pl.ds(x0, 2), other],
            dst_ref=sib_buf.at[h, yy, pl.ds(x0, 2)],
            send_sem=sib_ss.at[h, zz], recv_sem=sib_rs.at[h, zz],
            device_id=sib, device_id_type=MESH,
        )

    def consume(u):
        h, zz = block(u)
        yy, x0 = zz // 2, (zz % 2) * 2
        pt = p_all[h, zz]
        part = dot_tn(win_s[...], pt)
        ipart[h, yy, x0] = part[:, 0:TB].astype(bf16)
        ipart[h, yy, x0 + 1] = part[:, TB:2 * TB].astype(bf16)
        sib_copy(h, zz).start()

        @pl.when(u < 14)
        def _():
            wgrad_block(acc_in, p_all, x_all, u)

    def join(u):
        h, zz = block(u)
        yy, x0 = zz // 2, (zz % 2) * 2
        sib_copy(h, zz).wait_recv()
        for q in range(2):
            ipart[h, yy, x0 + q, half, :] = (
                ipart[h, yy, x0 + q, half, :].astype(f32) + sib_buf[h, yy, x0 + q].astype(f32)
            ).astype(bf16)

    def p_step(u, _):
        @pl.when(u >= 4)
        def _():
            ag_wait(*pg, u)

        @pl.when((u >= 4) & (u < 14))
        def _():
            ag_copy(*pg, u + 4).start()

        @pl.when(u >= 14)
        def _():
            ag_wait(*act, u - 4)
            ag_copy(*act, u).start()

        consume(u)

        @pl.when(u == 3)
        def _():
            ag_copy(*pg, 6).start()
            ag_copy(*pg, 7).start()

        @pl.when(u >= 5)
        def _():
            join(u - 3)

        return 0

    lax.fori_loop(2, 18, p_step, 0)

    def join_step(u, _):
        join(u)
        return 0

    lax.fori_loop(15, 18, join_step, 0)

    def feature_rows(off, size):
        return pl.ds(pl.multiple_of(base + off, 16), size)

    a_rows, b_rows = feature_rows(0, QUART), feature_rows(QUART, QUART)
    au, av = feature_rows(0, EIGHTH), feature_rows(EIGHTH, EIGHTH)
    bu, bv = feature_rows(QUART, EIGHTH), feature_rows(QUART + EIGHTH, EIGHTH)

    def add_to(view, *others):
        v = view[...].astype(f32)
        for o in others:
            v += o[...].astype(f32)
        view[...] = v.astype(bf16)

    def ring4(slab, off, devs, ru, rv, rp, rm, rows_all, rows_u, rows_v):
        def s1():
            return [
                start(slab(off(2), rows_u), ru, devs[1]),
                start(slab(off(2), rows_v), rv, devs[-1]),
            ]

        def s2(ids):
            arrived(ids[0], ru)
            add_to(slab(off(1), rows_u), ru)
            out = [start(slab(off(1), rows_all), rp, devs[1])]
            arrived(ids[1], rv)
            add_to(slab(off(-1), rows_v), rv)
            return out + [start(slab(off(-1), rows_all), rm, devs[-1])]

        def s3(ids):
            arrived(ids[0], rp)
            arrived(ids[1], rm)
            add_to(slab(off(0), rows_all), rp, rm)

        return s1, s2, s3

    ya = ring4(lambda o, rr: ipart.at[:, o, :, rr], yo, ydev, y_u, y_v, y_p, y_m, a_rows, au, av)
    xb = ring4(lambda o, rr: ipart.at[:, :, o, rr], xo, xdev, x_u, x_v, x_p, x_m, b_rows, bu, bv)
    xa = ring4(lambda o, rr: ipart.at[:, y, o, rr], xo, xdev, a2u, a2v, a2p, a2m, a_rows, au, av)
    yb = ring4(lambda o, rr: ipart.at[:, o, x, rr], yo, ydev, b2u, b2v, b2p, b2m, b_rows, bu, bv)

    i1, i2 = ya[0](), xb[0]()

    def square_sums(acc, off_row, off_col):
        total = jnp.zeros((FB, 1), f32)
        for q in range(5):
            c = slice(q * TB, (q + 1) * TB)
            v = acc[:, c]
            v = v * v
            col_st[0:1, off_col + q * TB:off_col + (q + 1) * TB] = jnp.sum(v, axis=0, keepdims=True)
            total += jnp.sum(v, axis=1, keepdims=True)
        tr_s[0:FB, :] = jnp.broadcast_to(total, (FB, TB))
        row_st[0:1, off_row:off_row + 512] = jnp.transpose(tr_s[...])[0:1, :]

    def wgrad_step(u, _):
        wgrad_block(acc_out, act_all, g_all, u)
        return 0

    def wgrad_in_step(u, _):
        wgrad_block(acc_in, p_all, x_all, u)
        return 0

    lax.fori_loop(14, 18, wgrad_in_step, 0)
    square_sums(acc_in, 0, 0)
    i1, i2 = ya[1](i1), xb[1](i2)
    lax.fori_loop(10, 14, wgrad_step, 0)

    def act_last(u, _):
        ag_wait(*act, u)
        wgrad_block(acc_out, act_all, g_all, u)
        return 0

    lax.fori_loop(14, 18, act_last, 0)
    square_sums(acc_out, 512, 640)

    xk_slots = [xo(-(o // 2)) * 2 + (k + o) % 2 for o in range(1, 8)]
    y_slots = [yo(-o) for o in range(1, 4)]
    z_slots = [zo(-o) for o in range(1, 8)]

    def exchange(src, rx, me, peers):
        rx[me] = src[...]
        return [start(src, rx.at[me], p) for p in peers]

    def collect(ids, rx, slots, n):
        for i, slot in zip(ids, slots):
            arrived(i, rx.at[slot])
        total = rx[0]
        for j in range(1, n):
            total += rx[j]
        return total

    col_ids = exchange(col_st, col_rx, x * 2 + k, xk_peers)
    row_ids = exchange(row_st, row_rx, z, z_peers)

    def drain(u, _):
        ag_copy(*act, u).wait_send()
        ag_copy(*pg, u).wait_send()
        rs_copy(rs_buf.at[u - 4], u).wait_send()
        return 0

    lax.fori_loop(4, 18, drain, 0)

    def sib_drain(i, _):
        sib_copy(i // 8, i % 8).wait_send()
        return 0

    lax.fori_loop(0, 16, sib_drain, 0)
    early = len(sent)
    for cp in sent[:early - 18]:
        cp.wait_send()
    ya[2](i1)
    xb[2](i2)
    i1, i2 = xa[0](), yb[0]()
    for name in ("rip", "rop", "cip", "cop"):
        loads[name].wait()
    col2_st[...] = collect(col_ids, col_rx, xk_slots, 8)
    col_ids = exchange(col2_st, col2_rx, y, y_peers)
    i1, i2 = xa[1](i1), yb[1](i2)
    row_sum = collect(row_ids, row_rx, z_slots, 8)

    def moment(prev, part, n):
        prev = prev[...].reshape(1, prev.shape[0])
        return decay_rate * prev + (1.0 - decay_rate) * (part / n + epsilon_sq)

    rows_o[...] = jnp.ones_like(rows_o)
    rows_o[0:1, 0:FB] = moment(rip_s, row_sum[:, 0:FB], D)
    rows_o[0:1, 512:512 + FB] = moment(rop_s, row_sum[:, 512:512 + FB], D)
    row_f = 1.0 / jnp.sqrt(rows_o[...])
    col_sum = collect(col_ids, col2_rx, y_slots, 4)
    cols_o[0:1, 0:DB] = moment(cip_s, col_sum[:, 0:DB], FF)
    cols_o[0:1, DB:2 * DB] = moment(cop_s, col_sum[:, DB:2 * DB], FF)
    root_tokens = math.sqrt(TOKENS)

    stores = []

    def store(src, dst):
        cp = pltpu.make_async_copy(src, dst, io_sem.at[9 + len(stores)])
        cp.start()
        stores.append(cp)

    store(rows_o, rows_ref)
    store(cols_o, cols_ref)

    def raw_update(acc, out_ref, row_part, col, off):
        rows = jnp.transpose(jnp.broadcast_to(row_part, (TB, 512)))[0:FB, :]
        factor = root_tokens / jnp.sqrt(col)
        total = jnp.zeros((1, TB), f32)
        for q in range(5):
            c = slice(q * TB, (q + 1) * TB)
            v = acc[:, c] * (rows * factor[:, c])
            acc[:, c] = v
            total += jnp.sum(v * v, axis=0, keepdims=True)
        sc_st[0:1, off:off + TB] = total
        store(acc, out_ref)

    raw_update(acc_in, ui_ref, row_f[:, 0:512], cols_o[0:1, 0:DB], 0)
    raw_update(acc_out, uo_ref, row_f[:, 512:1024], cols_o[0:1, DB:2 * DB], TB)
    sc_ids = exchange(sc_st, sc_rx1, x * 2 + k, xk_peers)
    xa[2](i1)
    yb[2](i2)
    fin = start(ipart.at[1 - k, y, x, half], fin_buf, sib)
    sc2_st[...] = collect(sc_ids, sc_rx1, xk_slots, 8)
    sc_ids = exchange(sc2_st, sc_rx2, y, y_peers)
    out_s[half, :] = ipart[k, y, x, half, :].astype(f32)
    arrived(fin, fin_buf)
    out_s[other, :] = fin_buf[...].astype(f32)
    for q in range(5):
        c = slice(q * TB, (q + 1) * TB)
        ig_s[:, c] = jnp.transpose(out_s[c, :]).astype(bf16)
    store(ig_s, ig_ref)
    sc3_st[...] = collect(sc_ids, sc_rx2, y_slots, 4)
    sc_ids = exchange(sc3_st, sc_rx3, z, z_peers)
    sums_o[...] = collect(sc_ids, sc_rx3, z_slots, 8)
    store(sums_o, sums_ref)
    for cp in sent[early - 18:]:
        cp.wait_send()
    for cp in stores:
        cp.wait()


def finish(
    ig_in, ui_in, uo_in, rows, cols, sums,
    ig_ref, ui_ref, ri_ref, ci_ref, uo_ref, ro_ref, co_ref,
):
    ig_ref[...] = ig_in[...]

    def clip(raw, out_ref, part):
        total = jnp.sum(part, axis=1, keepdims=True)
        rms = jnp.sqrt(total / (FF * D))
        out_ref[...] = raw[...] * (1.0 / jnp.maximum(1.0, rms / clip_limit))

    clip(ui_in, ui_ref, sums[0:1, 0:TB])
    clip(uo_in, uo_ref, sums[0:1, TB:2 * TB])
    ri_ref[...] = rows[0:1, 0:FB].reshape(FB)
    ro_ref[...] = rows[0:1, 512:512 + FB].reshape(FB)
    ci_ref[...] = cols[0:1, 0:DB].reshape(DB)
    co_ref[...] = cols[0:1, DB:2 * DB].reshape(DB)


COPIES = 128


def per_device(
    inputs, grad_out, pre_act, w_in, w_out, row_in_prev, col_in_prev, row_out_prev, col_out_prev
):
    hbm = pl.BlockSpec(memory_space=pl.ANY)
    strip = pl.BlockSpec((FB // 3, DB), lambda i: (i, 0))

    def whole(*shape):
        return pl.BlockSpec(shape, lambda i: (0,) * len(shape))

    dma = pltpu.SemaphoreType.DMA

    def v(*shape, dtype=bf16):
        return pltpu.VMEM(shape, dtype)

    ig, ui, uo, rows, cols, sums = pl.pallas_call(
        kernel,
        out_shape=(
            jax.ShapeDtypeStruct((TB, DB), bf16),
            jax.ShapeDtypeStruct((FB, DB), f32),
            jax.ShapeDtypeStruct((FB, DB), f32),
            jax.ShapeDtypeStruct((1, 1024), f32),
            jax.ShapeDtypeStruct((1, 1280), f32),
            jax.ShapeDtypeStruct((1, 256), f32),
        ),
        in_specs=[hbm] * 9,
        out_specs=[hbm] * 6,
        scratch_shapes=[
            v(2, 4, 4, TB, DB), v(2, 4, 4, TB, DB),
            v(2, 8, FB, 256), v(2, 8, FB, 256),
            v(2, FB, 256, dtype=f32),
            v(2, 8, FB, 256),
            v(14, FB, 256),
            v(FB, 512), v(FB, DB), v(FB, DB),
            v(512, TB, dtype=f32),
            v(FB, DB, dtype=f32), v(FB, DB, dtype=f32),
            v(2, 4, 4, DB, TB), v(2, 4, 4, HALF, TB),
            v(2, 4, EIGHTH, TB), v(2, 4, EIGHTH, TB), v(2, 4, QUART, TB), v(2, 4, QUART, TB),
            v(2, 4, EIGHTH, TB), v(2, 4, EIGHTH, TB), v(2, 4, QUART, TB), v(2, 4, QUART, TB),
            v(2, EIGHTH, TB), v(2, EIGHTH, TB), v(2, QUART, TB), v(2, QUART, TB),
            v(2, EIGHTH, TB), v(2, EIGHTH, TB), v(2, QUART, TB), v(2, QUART, TB),
            v(HALF, TB), v(DB, TB, dtype=f32), v(TB, DB),
            v(FB, dtype=f32), v(DB, dtype=f32), v(FB, dtype=f32), v(DB, dtype=f32),
            v(1, 1024, dtype=f32), v(1, 1280, dtype=f32), v(1, 256, dtype=f32),
            v(1, 1024, dtype=f32), v(8, 1, 1024, dtype=f32),
            v(1, 1280, dtype=f32), v(8, 1, 1280, dtype=f32),
            v(1, 1280, dtype=f32), v(4, 1, 1280, dtype=f32),
            v(1, 256, dtype=f32), v(1, 256, dtype=f32), v(1, 256, dtype=f32),
            v(8, 1, 256, dtype=f32), v(4, 1, 256, dtype=f32), v(8, 1, 256, dtype=f32),
            dma((COPIES,)), dma((COPIES,)), dma((2, 8)), dma((2, 8)),
            dma((18,)), dma((18,)), dma((18,)), dma((18,)), dma((18,)), dma((18,)), dma((16,)),
        ],
        compiler_params=pltpu.CompilerParams(
            collective_id=0, has_side_effects=True, vmem_limit_bytes=60 * 1024 * 1024
        ),
        name="ffn_backward",
    )(
        inputs, grad_out, pre_act.T, w_in, w_out,
        row_in_prev, col_in_prev, row_out_prev, col_out_prev,
    )
    return pl.pallas_call(
        finish,
        out_shape=(
            jax.ShapeDtypeStruct((TB, DB), bf16),
            jax.ShapeDtypeStruct((FB, DB), f32),
            jax.ShapeDtypeStruct((FB,), f32),
            jax.ShapeDtypeStruct((DB,), f32),
            jax.ShapeDtypeStruct((FB, DB), f32),
            jax.ShapeDtypeStruct((FB,), f32),
            jax.ShapeDtypeStruct((DB,), f32),
        ),
        grid=(3,),
        in_specs=[whole(TB, DB), strip, strip, whole(1, 1024), whole(1, 1280), whole(1, 256)],
        out_specs=[whole(TB, DB), strip, whole(FB), whole(DB), strip, whole(FB), whole(DB)],
        compiler_params=pltpu.CompilerParams(vmem_limit_bytes=60 * 1024 * 1024),
        name="clip_updates",
    )(ig, ui, uo, rows, cols, sums)


def solution(mesh):
    return jax.shard_map(
        per_device,
        mesh=mesh,
        in_specs=(
            P("row", "col"),
            P("row", "col"),
            P("col", "row"),
            P("row", "col"),
            P("row", "col"),
            P("row"),
            P("col"),
            P("row"),
            P("col"),
        ),
        out_specs=(
            P("row", "col"),
            P("row", "col"),
            P("row"),
            P("col"),
            P("row", "col"),
            P("row"),
            P("col"),
        ),
        check_vma=False,
    )
```
